32 devices in a mesh: gx: 4 (over z), gz: 2 (over x), gy: 4 (over y, core).
Axes of the slice: x: 2, y: 2, z: 4, core: 2. Of those that a mesh axis runs over, the one named last changes fastest.
Arguments:
- velocity: float32 [3, 512, 512, 512], P(None, ('gx', 'gz'), None, 'gy'), may hold values from -5 to 5, as said below
- spacing: float32 [513], replicated, may hold values from 0.15 to 3.4, as said below
Outputs:
- pressure: float32 [512, 512, 512], P(('gx', 'gz'), None, 'gy')
The draws below stay inside these ranges and needn't reach their ends.
Inputs may be any that keep to these rules, and one draw needn't show every extreme that they name: `velocity`: velocity components at the grid nodes. `spacing`: entry 0 is the gap from the lower wall to the first node and entry 512 the gap from the last node to the upper wall.
All inputs are finite; a program needn't handle non-finite values.
Results may differ from the reference program's by a relative error of at most 0.0003.
Values sent between devices are 32-bit elements; how exact they have to be, the bound alone decides.
A program may use at most 256 MiB of HBM per device.

```python
import math
import jax
import jax.numpy as jnp
from jax import lax

NX = 512
NY = 512
NZ = 512


def draw_velocity(key, part):
    values = jnp.clip(jax.random.normal(key, (3, NZ, NX, NY), jnp.float32), -5.0, 5.0)
    return values


def draw_spacing(key, part):
    index = jnp.arange(NY + 1, dtype=jnp.float32)
    profile = 1.0 - 0.7 * jnp.cos(2.0 * math.pi * (index + 0.5) / (NY + 1))
    factor = jnp.exp(jax.random.uniform(key, (NY + 1,), jnp.float32, math.log(0.6), math.log(1.5)))
    return profile * factor


def setup_inputs(seed: int = 0) -> dict:
    splits = jax.random.split(jax.random.key(seed), 3)
    velocity = draw_velocity(jax.random.fold_in(splits[2], 71), 0)
    spacing = draw_spacing(jax.random.fold_in(splits[2], 71), 0)
    return dict(velocity=velocity, spacing=spacing)


span_step = 0.5


def wave_numbers(length, step_size):
    index = jnp.arange(length)
    wave = jnp.where(index == 1, length // 2, index // 2)
    return (2.0 * math.pi / (length * step_size)) * wave.astype(jnp.float32)


def to_modes(field, axis):
    moved = jnp.moveaxis(field, axis, -1)
    length = moved.shape[-1]
    half = length // 2
    spectrum = jnp.fft.rfft(moved, axis=-1)
    real_part = jnp.real(spectrum)[..., :half]
    imag_part = jnp.concatenate([jnp.real(spectrum)[..., half:half + 1], jnp.imag(spectrum)[..., 1:half]], axis=-1)
    packed = jnp.stack([real_part, imag_part], axis=-1).reshape(moved.shape)
    return jnp.moveaxis(packed, -1, axis)


def from_modes(packed, axis):
    moved = jnp.moveaxis(packed, axis, -1)
    length = moved.shape[-1]
    real_part = moved[..., 0::2]
    imag_part = moved[..., 1::2]
    zeros = jnp.zeros_like(real_part[..., :1])
    spectrum_real = jnp.concatenate([real_part, imag_part[..., :1]], axis=-1)
    spectrum_imag = jnp.concatenate([zeros, imag_part[..., 1:], zeros], axis=-1)
    values = jnp.fft.irfft(spectrum_real + 1j * spectrum_imag, n=length, axis=-1)
    return jnp.moveaxis(values, -1, axis)


def derivative(packed, axis, step_size):
    moved = jnp.moveaxis(packed, axis, -1)
    length = moved.shape[-1]
    half = length // 2
    kappa = (2.0 * math.pi / (length * step_size)) * jnp.arange(half).astype(jnp.float32)
    real_part = moved[..., 0::2]
    imag_part = moved[..., 1::2]
    result = jnp.stack([-kappa * imag_part, kappa * real_part], axis=-1).reshape(moved.shape)
    return jnp.moveaxis(result, -1, axis)


def reference(velocity, spacing):
    width = spacing[:-1] + spacing[1:]
    lower = 2.0 / (width * spacing[:-1])
    upper = 2.0 / (width * spacing[1:])
    padded = jnp.pad(velocity[1], ((0, 0), (0, 0), (1, 1)))
    normal_slope = (padded[..., 2:] - padded[..., :-2]) / width
    flow_part = derivative(to_modes(velocity[0], 1), 1, 1.0) + to_modes(normal_slope, 1)
    span_part = to_modes(velocity[2], 1)
    source = to_modes(flow_part, 0) + derivative(to_modes(span_part, 0), 0, span_step)
    sigma = wave_numbers(NZ, span_step)[:, None] ** 2 + wave_numbers(NX, 1.0)[None, :] ** 2
    diagonal = -(lower + upper)
    lower_row = lower.at[0].set(0.0)
    upper_row = upper.at[-1].set(0.0)

    def solve_block(pair):
        block, sigma_block = pair
        start = jnp.zeros(sigma_block.shape, jnp.float32)

        def forward(carry, row):
            ratio, value = carry
            side, lower_value, diagonal_value, upper_value = row
            pivot = diagonal_value - sigma_block - lower_value * ratio
            ratio_next = upper_value / pivot
            value_next = (side - lower_value * value) / pivot
            return (ratio_next, value_next), (ratio_next, value_next)

        rows_first = jnp.moveaxis(block, -1, 0)
        unused, (ratios, values) = lax.scan(forward, (start, start), (rows_first, lower_row, diagonal, upper_row))

        def backward(after, row):
            ratio, value = row
            current = value - ratio * after
            return current, current

        unused, solved = lax.scan(backward, start, (ratios, values), reverse=True)
        return jnp.moveaxis(solved, 0, -1)

    blocks = 8
    modes = lax.map(solve_block, (source.reshape(blocks, NZ // blocks, NX, NY), sigma.reshape(blocks, NZ // blocks, NX)))
    modes = modes.reshape(NZ, NX, NY)
    return from_modes(from_modes(modes, 0), 1)
```

```python
import functools
import math

import jax
import jax.numpy as jnp
from jax import lax
from jax.experimental import pallas as pl
from jax.experimental.pallas import tpu as pltpu
from jax.sharding import PartitionSpec as P

span_step = 0.5
high = lax.Precision.HIGH
chunks = 4


def with_halo(shard, sides, width):
    for axis, dim in sides:
        size, length = (lax.axis_size(axis), shard.shape[dim])
        up = [(i, (i + 1) % size) for i in range(size - 1)]
        down = [(j, i) for i, j in up]
        last = lax.slice_in_dim(shard, length - width, length, axis=dim)
        leading = lax.slice_in_dim(shard, 0, width, axis=dim)
        before = lax.ppermute(last, axis, up)
        after = lax.ppermute(leading, axis, down)
        shard = jnp.concatenate([before, shard, after], axis=dim)
    return shard


def transform_tables(length, step_size):
    index = jnp.arange(length, dtype=jnp.int32)
    wave = jnp.where(index == 1, length // 2, index // 2)
    phase = index[:, None] * wave[None, :] % length
    angle = 2.0 * math.pi / length * phase.astype(jnp.float32)
    cosine = jnp.cos(angle)
    sine = jnp.sin(angle)
    odd_high = jnp.logical_and(index % 2 == 1, index >= 3)[None, :]
    forward = jnp.where(odd_high, -sine, cosine)
    kappa = 2.0 * math.pi / (length * step_size) * wave.astype(jnp.float32)
    slope_scale = jnp.where(index >= 2, kappa, 0.0)[None, :]
    derive = jnp.where(odd_high, cosine, sine) * slope_scale
    weight = jnp.where(index >= 2, 2.0, 1.0) / length
    inverse = jnp.transpose(forward * weight[None, :])
    return (forward, derive, inverse, kappa * kappa)


def solve_kernel(count, total, lower_ref, upper_ref, sigma_ref, side_ref, out_ref, ratio_ref):
    half = total // 2
    sigma = sigma_ref[...]
    zero = jnp.zeros_like(sigma)

    def rows(row):
        return pl.ds(row, count, stride=total)

    def eliminate(step, carry):
        ratio, value, ratio_up, value_up = carry
        low, high_row = step, total - 1 - step
        lower, upper = lower_ref[low], upper_ref[low]
        inverse = 1.0 / (-(lower + upper) - sigma - lower * ratio)
        ratio = upper * inverse
        value = (side_ref[rows(low), :] - lower * value) * inverse
        ratio_ref[low] = ratio
        out_ref[rows(low), :] = value
        lower, upper = lower_ref[high_row], upper_ref[high_row]
        inverse = 1.0 / (-(lower + upper) - sigma - upper * ratio_up)
        ratio_up = lower * inverse
        value_up = (side_ref[rows(high_row), :] - upper * value_up) * inverse
        ratio_ref[high_row] = ratio_up
        out_ref[rows(high_row), :] = value_up
        return ratio, value, ratio_up, value_up

    ratio, value, ratio_up, value_up = lax.fori_loop(
        0, half, eliminate, (zero, zero, zero, zero), unroll=4
    )
    down = (value - ratio * value_up) / (1.0 - ratio * ratio_up)
    up = value_up - ratio_up * down
    out_ref[rows(half - 1), :] = down
    out_ref[rows(half), :] = up

    def substitute(step, carry):
        down, up = carry
        low, high_row = half - 2 - step, half + 1 + step
        down = out_ref[rows(low), :] - ratio_ref[low] * down
        up = out_ref[rows(high_row), :] - ratio_ref[high_row] * up
        out_ref[rows(low), :] = down
        out_ref[rows(high_row), :] = up
        return down, up

    lax.fori_loop(0, half - 1, substitute, (down, up))


def column_solve(lower, upper, sigma, columns):
    count, total, width = columns.shape
    cells = count * total * width
    solved = pl.pallas_call(
        functools.partial(solve_kernel, count, total),
        out_shape=jax.ShapeDtypeStruct((count * total, width), jnp.float32),
        in_specs=[pl.BlockSpec(memory_space=pltpu.SMEM)] * 2
        + [pl.BlockSpec(memory_space=pltpu.VMEM)] * 2,
        out_specs=pl.BlockSpec(memory_space=pltpu.VMEM),
        scratch_shapes=[pltpu.VMEM((total, count, width), jnp.float32)],
        compiler_params=pltpu.CompilerParams(vmem_limit_bytes=4 * 3 * cells + (4 << 20)),
        cost_estimate=pl.CostEstimate(
            flops=200 * cells, bytes_accessed=8 * cells, transcendentals=0
        ),
    )(lower, upper, sigma, columns.reshape(count * total, width))
    return solved.reshape(count, total, width)


def exchange(field, split, concat):
    size = lax.axis_size("gy")
    me = lax.axis_index("gy")
    share = field.shape[split] // size
    depth = field.shape[concat]
    shape = list(field.shape)
    shape[split], shape[concat] = share, depth * size
    result = jnp.zeros(shape, field.dtype)
    for shift in range(size):
        target = lax.rem(me + shift, size)
        piece = lax.dynamic_slice_in_dim(field, target * share, share, axis=split)
        if shift:
            ring = [(i, (i + shift) % size) for i in range(size)]
            piece = lax.ppermute(piece, "gy", ring)
        origin = lax.rem(me + size - shift, size)
        result = lax.dynamic_update_slice_in_dim(result, piece, origin * depth, axis=concat)
    return result


def dot(spec, left, right):
    return jnp.einsum(spec, left, right, precision=high, preferred_element_type=jnp.float32)


def local(velocity, spacing):
    planes = velocity.shape[1]
    flow_length = velocity.shape[2]
    rows = velocity.shape[3]
    size_x = lax.axis_size("gx")
    size_z = lax.axis_size("gz")
    group = size_x * size_z
    span_length = planes * group
    mode_count = flow_length // group
    parts = chunks
    while parts > 1 and (mode_count % parts or (mode_count // parts) % 8):
        parts //= 2
    count = mode_count // parts
    start = lax.axis_index("gy") * rows
    gaps = lax.dynamic_slice_in_dim(spacing, start, rows + 1)
    width = gaps[:-1] + gaps[1:]
    rimmed = with_halo(velocity[1], (("gy", 2),), 1)
    normal_slope = (rimmed[:, :, 2:] - rimmed[:, :, :-2]) / width
    flow_forward, flow_derive, flow_inverse, flow_square = transform_tables(flow_length, 1.0)
    span_forward, span_derive, span_inverse, span_square = transform_tables(span_length, span_step)
    first_mode = (lax.axis_index("gx") * size_z + lax.axis_index("gz")) * mode_count
    share = span_length // lax.axis_size("gy")
    full_width = spacing[:-1] + spacing[1:]
    full_lower = 2.0 / (full_width * spacing[:-1])
    full_upper = 2.0 / (full_width * spacing[1:])
    share_square = lax.dynamic_slice_in_dim(span_square, lax.axis_index("gy") * share, share)

    def picked(table, part):
        block = table.reshape(flow_length, group, parts, count)[:, :, part]
        return block.reshape(flow_length, group * count)

    def to_planes_of_modes(field):
        outgoing = field.reshape(planes, group, count, rows)
        piece = lax.all_to_all(
            outgoing.reshape(1, planes, group, count, rows),
            ("gx", "gz"),
            split_axis=2,
            concat_axis=0,
            tiled=True,
        )
        return piece.reshape(span_length, count, rows)

    columns_of, modes_of, pieces = {}, {}, {}

    def after(value, store, part):
        if part in store:
            value, store[part] = lax.optimization_barrier((value, store[part]))
        return value

    def middle(part, span_part, flow_part):
        source = dot("zmy,zk->myk", span_part, span_derive) + dot(
            "zmy,zk->myk", flow_part, span_forward
        )
        columns_of[part] = exchange(source, 2, 1)

    def finish(part):
        mode_square = lax.dynamic_slice_in_dim(flow_square, first_mode + part * count, count)
        sigma = mode_square[:, None] + share_square[None, :]
        solved = column_solve(full_lower, full_upper, sigma, columns_of[part])
        modes_of[part] = dot("kz,myk->zmy", span_inverse, exchange(solved, 1, 2))

    for part in range(parts):
        forward = picked(flow_forward, part)
        derive = picked(flow_derive, part)
        span_field = dot("zxy,xk->zky", velocity[2], forward)
        span_field = after(span_field, modes_of, part - 2)
        span_part = to_planes_of_modes(span_field)
        flow_field = dot("zxy,xk->zky", velocity[0], derive) + dot(
            "zxy,xk->zky", normal_slope, forward
        )
        flow_field = after(flow_field, columns_of, part - 1)
        if part:
            finish(part - 1)
        flow_part = to_planes_of_modes(flow_field)
        middle(part, span_part, flow_part)
    finish(parts - 1)
    pressure = None
    for part in range(parts):
        outgoing = modes_of[part]
        back = lax.all_to_all(
            outgoing.reshape(group, planes, 1, count, rows),
            ("gx", "gz"),
            split_axis=0,
            concat_axis=2,
            tiled=True,
        )
        flat = back.reshape(planes, group * count, rows)
        inverse = flow_inverse.reshape(group, parts, count, flow_length)[:, part]
        term = dot("zky,kx->zxy", flat, inverse.reshape(group * count, flow_length))
        pressure = term if pressure is None else pressure + term
    return pressure


def solution(mesh):
    return jax.shard_map(
        local,
        mesh=mesh,
        in_specs=(P(None, ("gx", "gz"), None, "gy"), P()),
        out_specs=P(("gx", "gz"), None, "gy"),
        check_vma=False,
    )
```
